32 devices in a mesh: member: 4 (over x, core), tile: 4 (over z), grp: 2 (over y).
Axes of the slice: x: 2, y: 2, z: 4, core: 2. Of those that a mesh axis runs over, the one named last changes fastest.
Arguments:
- members: float32 [80, 128, 1024], P(('member', 'grp'), 'tile'), may hold values from -6 to 6
- courant_x: float32 [128, 1024], P('tile'), may hold values from -0.48 to 0.48
- courant_y: float32 [128, 1024], P('tile'), may hold values from -0.48 to 0.48
- obs_cell: int32 [4, 8, 1024], P('tile', ('member', 'grp')), may hold values from 0 to 4095
- innovation: float32 [4, 8, 1024], P('tile', ('member', 'grp')), may hold values from -6 to 6
- obs_weight: float32 [4, 8, 1024], P('tile', ('member', 'grp')), may hold values from 0.5 to 3
- stencil_offsets: int32 [9, 2], replicated, may hold values from -2 to 2, as said below
- stencil_weights: float32 [9], replicated, may hold values from 0.2 to 1
Outputs:
- analysis: float32 [80, 128, 1024], P(('member', 'grp'), 'tile')
- increment: float32 [128, 1024], P('tile', ('member', 'grp'))
The draws below stay inside these ranges and needn't reach their ends.
Inputs may be any that keep to these rules, and one draw needn't show every extreme that they name: `stencil_offsets`: each row is a stencil entry's offsets along rows and columns; some entry reaches 2 cells along rows and some along columns. `obs_cell`: cells of a block are numbered row by row, 128 to a row.
All inputs are finite; a program needn't handle non-finite values.
Results may differ from the reference program's by a relative error of at most 0.0001.
Values sent between devices are 32-bit elements; how exact they have to be, the bound alone decides.
A program may use at most 128 MiB of HBM per device.

```python
import math
import jax
import jax.numpy as jnp
from jax import lax

CX = 32
CY = 128
RADIUS = 2
STENCIL_ENTRIES = 9
FSTEPS = 3
GSTEPS = 2
ENS = 80
NX = 128
NY = 1024
OBS_BLK = 1024
N_MEMBER = 4
N_TILE = 4
N_GRP = 2


def draw_stencil_offsets(key, part):
    first_key, second_key = jax.random.split(jax.random.fold_in(key, 17), 2)
    offsets = jax.random.randint(first_key, (STENCIL_ENTRIES, 2), -RADIUS, RADIUS + 1)
    signs = 2 * jax.random.randint(second_key, (2,), 0, 2) - 1
    offsets = offsets.at[0, 0].set(signs[0] * RADIUS)
    offsets = offsets.at[1, 1].set(signs[1] * RADIUS)
    return offsets.astype(jnp.int32)


def set_ends(values, stream_key, smallest, high):
    longest = values.shape.index(max(values.shape))
    spots = []
    for shift in (0, 1):
        where = [jax.random.randint(jax.random.fold_in(stream_key, axis), (), 0, length) for axis, length in enumerate(values.shape)]
        where[longest] = (where[longest] + shift) % values.shape[longest]
        spots.append(tuple(where))
    return values.at[spots[0]].set(smallest).at[spots[1]].set(high)


def levels(rng, dims, pieces, smallest, largest):
    factor_of, own = 1.0, jax.random.fold_in(rng, 6)
    for axis_at, blocks in pieces:
        steps = jnp.exp(jax.random.uniform(jax.random.fold_in(own, axis_at), (blocks,), jnp.float32, smallest / len(pieces), largest / len(pieces)))
        factor_of = factor_of * jnp.repeat(steps, dims[axis_at] // blocks).reshape([-1 if axis == axis_at else 1 for axis in range(len(dims))])
    return factor_of


def centred(own_key, dims, scale, reach, cuts=(), dtype=jnp.bfloat16):
    array = jax.random.normal(own_key, dims, jnp.float32) * scale
    if len(cuts) > 0:
        array = levels(own_key, dims, cuts, -0.22, 0.18) * array
    return jnp.clip(array, min=-reach, max=reach).astype(dtype)


def setup_inputs(seed: int = 0) -> dict:
    key_list = jax.random.split(jax.random.key(seed), 9)
    members = centred(key_list[0], (ENS, NX, NY), 1.0, 6.0, ((0, 8), (1, 4)), jnp.float32)
    courant_x = jnp.clip(jax.random.uniform(key_list[1], (NX, NY), jnp.float32, -0.48, 0.48) * levels(key_list[1], (NX, NY), ((0, 4),), -0.4, 0.0), -0.48, 0.48)
    courant_y = jnp.clip(jax.random.uniform(key_list[2], (NX, NY), jnp.float32, -0.48, 0.48) * levels(key_list[2], (NX, NY), ((0, 4),), -0.4, 0.0), -0.48, 0.48)
    obs_cell = set_ends(jax.random.randint(key_list[3], (N_TILE, N_MEMBER * N_GRP, OBS_BLK), 0, CX * CY), jax.random.fold_in(key_list[3], 1), 0, (CX * CY) - 1).astype(jnp.int32)
    innovation = centred(key_list[4], (N_TILE, N_MEMBER * N_GRP, OBS_BLK), 1.0, 6.0, ((0, 4), (1, 8)), jnp.float32)
    obs_weight = jnp.clip(jnp.exp(math.log(3.0) - 1.7917595 * jax.random.uniform(key_list[5], (N_TILE, N_MEMBER * N_GRP, OBS_BLK), jnp.float32) ** levels(key_list[5], (N_TILE, N_MEMBER * N_GRP, OBS_BLK), ((0, 4), (1, 8)), -0.2, 0.2)), 0.5, 3.0)
    stencil_offsets = draw_stencil_offsets(jax.random.fold_in(key_list[8], 71), 0)
    stencil_weights = jnp.clip(jnp.exp(jax.random.uniform(key_list[7], (STENCIL_ENTRIES,), jnp.float32, math.log(0.2), math.log(1.0))), 0.2, 1.0)
    return {"members": members, "courant_x": courant_x, "courant_y": courant_y, "obs_cell": obs_cell, "innovation": innovation, "obs_weight": obs_weight, "stencil_offsets": stencil_offsets, "stencil_weights": stencil_weights}


STEP_SIZE = 0.25

def upwind(padded, courant_x, courant_y):
    centre = padded[..., 1:-1, 1:-1]
    upper = padded[..., :-2, 1:-1]
    lower = padded[..., 2:, 1:-1]
    left_cell = padded[..., 1:-1, :-2]
    right_cell = padded[..., 1:-1, 2:]
    x_plus = jnp.maximum(courant_x, 0.0)
    x_minus = jnp.minimum(courant_x, 0.0)
    y_plus = jnp.maximum(courant_y, 0.0)
    y_minus = jnp.minimum(courant_y, 0.0)
    return centre - x_plus * (centre - upper) - x_minus * (lower - centre) - y_plus * (centre - left_cell) - y_minus * (right_cell - centre)

def localize(padded, offsets, weights, sign, row_count, col_count):
    summed = jnp.zeros(padded.shape[:-2] + (row_count, col_count), jnp.float32)
    for entry in range(offsets.shape[0]):
        shifted = lax.dynamic_slice_in_dim(padded, RADIUS + sign * offsets[entry, 0], row_count, padded.ndim - 2)
        shifted = lax.dynamic_slice_in_dim(shifted, RADIUS + sign * offsets[entry, 1], col_count, padded.ndim - 1)
        summed = summed + weights[entry] * shifted
    return summed / jnp.sum(weights)

def pad_margin(values):
    widths = [(0, 0)] * (values.ndim - 2) + [(RADIUS, RADIUS), (RADIUS, RADIUS)]
    return jnp.pad(values, widths)

def reference(members, courant_x, courant_y, obs_cell, innovation, obs_weight, stencil_offsets, stencil_weights):

    def advect_step(field):
        for section in range(FSTEPS):
            field = upwind(jnp.pad(field, 1), courant_x, courant_y)
        return field
    predict_members = lax.map(advect_step, members)
    member_fields = predict_members.shape[0]
    member_deviation = math.sqrt(member_fields - 1)
    ensemble_average = lax.optimization_barrier(jnp.sum(predict_members, axis=0)) / member_fields
    deviation_rows = jnp.concatenate([(predict_members - ensemble_average[None]) / member_deviation, jnp.ones_like(predict_members[:1])], axis=0)
    tile_ids = lax.broadcasted_iota(jnp.int32, obs_cell.shape, 0)
    block_ids = lax.broadcasted_iota(jnp.int32, obs_cell.shape, 1)
    row_ids = tile_ids * CX + obs_cell // CY
    col_ids = block_ids * CY + obs_cell % CY
    flat_index = (row_ids * NY + col_ids).reshape(-1).astype(jnp.int32)
    innov_flat = innovation.reshape(-1)
    weight_flat = obs_weight.reshape(-1)
    row_count, col_count = (NX, NY)

    def observe(values):
        flat = values.reshape(-1)
        misfit = weight_flat * (flat[flat_index] - innov_flat)
        return jnp.zeros_like(flat).at[flat_index].add(misfit).reshape(values.shape)

    def combine(control):
        localized = localize(pad_margin(control), stencil_offsets, stencil_weights, 1, row_count, col_count)
        return lax.optimization_barrier(jnp.sum(deviation_rows[:-1] * localized[:-1], axis=0)) + localized[-1]
    control = jnp.zeros_like(deviation_rows)
    for sweep in range(GSTEPS):
        if sweep == 0:
            current = jnp.zeros((row_count, col_count), jnp.float32)
        else:
            current = combine(control)
        residual_field = observe(current)
        product = pad_margin(deviation_rows * residual_field[None])
        descent = control + localize(product, stencil_offsets, stencil_weights, -1, row_count, col_count)
        control = control - STEP_SIZE * descent
    increment = combine(control)
    return (predict_members + increment[None], increment)
```

```python
import math

import jax
import jax.numpy as jnp
from jax import lax
from jax.sharding import PartitionSpec as P

RADIUS = 2
FSTEPS = 3
STEP_SIZE = 0.25
GROUP = ("member", "grp")


def halo(cells, axis, width, dim):
    count = lax.axis_size(axis)
    head = lax.slice_in_dim(cells, 0, width, axis=dim)
    tail = lax.slice_in_dim(cells, cells.shape[dim] - width, cells.shape[dim], axis=dim)
    above = lax.ppermute(tail, axis, [(i, i + 1) for i in range(count - 1)])
    below = lax.ppermute(head, axis, [(i + 1, i) for i in range(count - 1)])
    return jnp.concatenate([above, cells, below], axis=dim)


def upwind(q, cx, cy):
    rows = q.shape[1]
    c = q[:, 1:-1]
    left = jnp.pad(c, ((0, 0), (0, 0), (1, 0)))[:, :, :-1]
    right = jnp.pad(c, ((0, 0), (0, 0), (0, 1)))[:, :, 1:]
    return (
        c
        - jnp.maximum(cx, 0.0) * (c - q[:, : rows - 2])
        - jnp.minimum(cx, 0.0) * (q[:, 2:] - c)
        - jnp.maximum(cy, 0.0) * (c - left)
        - jnp.minimum(cy, 0.0) * (right - c)
    )


def spread_out(f, taps, sign):
    rows = f.shape[1] - 2 * RADIUS
    cols = f.shape[2]
    g = jnp.pad(f, ((0, 0), (0, 0), (RADIUS, RADIUS)))
    total = 0.0
    for r in range(-RADIUS, RADIUS + 1):
        for c in range(-RADIUS, RADIUS + 1):
            part = g[:, RADIUS + sign * r : RADIUS + sign * r + rows, RADIUS + sign * c : RADIUS + sign * c + cols]
            total = total + taps[r + RADIUS, c + RADIUS] * part
    return total


def on_device(members, courant_x, courant_y, obs_cell, innovation, obs_weight, offsets, weights):
    n, rows, cols = members.shape
    reach = 2 * RADIUS
    edge = reach + FSTEPS
    groups = lax.axis_size(GROUP)
    total = n * groups
    tile = lax.axis_index("tile")
    tiles = lax.axis_size("tile")

    packed = halo(jnp.concatenate([members, courant_x[None], courant_y[None]]), "tile", edge, 1)
    q, cx, cy = packed[:n], packed[n], packed[n + 1]
    for s in range(FSTEPS):
        lo, hi = s + 1, rows + 2 * edge - s - 1
        q = upwind(q, cx[lo:hi], cy[lo:hi])
    fields = q[:, reach : reach + rows]

    own = jnp.sum(q, axis=0) / n
    mean = lax.psum(own, GROUP) / groups
    dev = (q - own[None]) / math.sqrt(total - 1)
    shift = (own - mean) * math.sqrt(n / (total - 1))
    ones = jnp.full_like(own, 1.0 / math.sqrt(groups))
    dev = jnp.concatenate([dev, shift[None], ones[None]])

    kr = jnp.arange(-RADIUS, RADIUS + 1)
    hit = (offsets[:, 0][:, None, None] == kr[None, :, None]) & (offsets[:, 1][:, None, None] == kr[None, None, :])
    taps = jnp.sum(jnp.where(hit, weights[:, None, None], 0.0), axis=0) / jnp.sum(weights)

    at = jnp.arange(rows + 2 * RADIUS) - RADIUS + tile * rows
    inside = ((at >= 0) & (at < tiles * rows)).astype(jnp.float32)[None, :, None]

    def apply(h):
        z = spread_out(dev * h[None], taps, -1) * inside
        y = spread_out(z, taps, 1)
        return jnp.sum(dev[:, reach : reach + rows] * y, axis=0) * -STEP_SIZE

    width = cols // groups
    cell = obs_cell.reshape(-1)
    w = obs_weight.reshape(-1)
    wi = w * innovation.reshape(-1)
    pick_r = (cell[None] // width == jnp.arange(rows)[:, None]).astype(jnp.float32)
    pick_c = (cell[:, None] % width == jnp.arange(width)[None]).astype(jnp.float32)
    both = jnp.dot(
        jnp.concatenate([pick_r * w[None], pick_r * wi[None]]), pick_c, precision=lax.Precision.HIGHEST
    )
    dense_w, dense_wi = both[:rows], both[rows:]

    def gathered(block):
        return halo(lax.all_gather(block, GROUP, axis=1, tiled=True), "tile", reach, 0)

    x0 = lax.psum_scatter(apply(gathered(-dense_wi)), GROUP, scatter_dimension=1, tiled=True)
    g1 = dense_w * x0 - dense_wi
    x1 = lax.psum_scatter(apply(gathered(g1)), GROUP, scatter_dimension=1, tiled=True)
    block = (1.0 - STEP_SIZE) * x0 + x1
    full = lax.all_gather(block, GROUP, axis=1, tiled=True)
    return fields + full[None], block


def solution(mesh):
    placed = (
        P(GROUP, "tile", None),
        P("tile", None),
        P("tile", None),
        P("tile", GROUP, None),
        P("tile", GROUP, None),
        P("tile", GROUP, None),
        P(),
        P(),
    )
    return jax.shard_map(
        on_device,
        mesh=mesh,
        in_specs=placed,
        out_specs=(P(GROUP, "tile", None), P("tile", GROUP)),
        check_vma=False,
    )
```

```python
import functools
import math

import jax
import jax.numpy as jnp
from jax import lax
from jax.experimental import pallas as pl
from jax.experimental.pallas import tpu as pltpu
from jax.sharding import PartitionSpec as P

RADIUS = 2
FSTEPS = 3
STEP_SIZE = 0.25
GROUP = ("member", "grp")
MESH = pl.DeviceIdType.MESH
SUB = 8
LANES = 128
REACH = 2 * RADIUS
SHIFTS = tuple(range(-RADIUS, RADIUS + 1))


def remote(src, dst, send_sem, recv_sem, where):
    return pltpu.make_async_remote_copy(
        src_ref=src, dst_ref=dst, send_sem=send_sem, recv_sem=recv_sem, device_id=where, device_id_type=MESH
    )


def moved(blocks, c, lane):
    if c == 0:
        return blocks
    turned = [pltpu.roll(x, (-c) % LANES, 1) for x in blocks]
    nothing = jnp.zeros_like(blocks[0])
    out = []
    for b in range(len(blocks)):
        if c > 0:
            other = turned[b + 1] if b + 1 < len(blocks) else nothing
            out.append(jnp.where(lane >= LANES - c, other, turned[b]))
        else:
            other = turned[b - 1] if b > 0 else nothing
            out.append(jnp.where(lane < -c, other, turned[b]))
    return out


def kernel(
    shape,
    offs, wts, members, cx_hbm, cy_hbm, cell_ref, innov_ref, weight_ref,
    out_hbm, inc_ref,
    Q, C, T1, T2, D, OWN, MR, MB, MG, OBW, OBI, G0, G1,
    M0, U0, L0, M1, U1, L1, H, U, Z, ACC, XP, X0, R0, R1, NB, NM,
    in_sem, out_sem, hs, hr, s0, r0, s1, r1, sm1, rm1, sm2, rm2, sx0, rx0, sx1, rx1, sn, rn,
):
    n, rows, groups, n_grp = shape
    total = n * groups
    tiles = lax.axis_size("tile")
    tile = lax.axis_index("tile")
    me = lax.axis_index("member") * n_grp + lax.axis_index("grp")
    has_up = tile > 0
    has_down = tile < tiles - 1
    top = 2 * SUB
    tall = rows + 2 * REACH
    lane = lax.broadcasted_iota(jnp.int32, (SUB, LANES), 1)
    blocks = range(groups)

    def at(p, t=None):
        where = {"member": p // n_grp, "grp": lax.rem(p, n_grp)}
        if t is not None:
            where["tile"] = t
        return where

    def partner(d):
        return lax.rem(me + d, groups)

    def sender(d):
        return lax.rem(me + groups - d, groups)

    def loads():
        for b in blocks:
            cols = pl.ds(b * LANES, LANES)
            yield pltpu.make_async_copy(cx_hbm.at[:, cols], Q.at[n, b, pl.ds(top, rows)], in_sem.at[1, b])
            yield pltpu.make_async_copy(cy_hbm.at[:, cols], Q.at[n + 1, b, pl.ds(top, rows)], in_sem.at[2, b])
        for b in blocks:
            cols = pl.ds(b * LANES, LANES)
            yield pltpu.make_async_copy(members.at[:, :, cols], Q.at[pl.ds(0, n), b, pl.ds(top, rows)], in_sem.at[0, b])

    for copy in loads():
        copy.start()

    barrier = pltpu.get_barrier_semaphore()
    for d in range(1, groups):
        pl.semaphore_signal(barrier, inc=1, device_id=at(partner(d)), device_id_type=MESH)

    @pl.when(has_up)
    def _():
        for d in blocks:
            pl.semaphore_signal(barrier, inc=1, device_id=at(partner(d), tile - 1), device_id_type=MESH)

    @pl.when(has_down)
    def _():
        for d in blocks:
            pl.semaphore_signal(barrier, inc=1, device_id=at(partner(d), tile + 1), device_id_type=MESH)

    sides = jnp.where(has_up, 1, 0) + jnp.where(has_down, 1, 0)
    for m in range(3):
        @pl.when(sides == m)
        def _(m=m):
            pl.semaphore_wait(barrier, groups - 1 + m * groups)

    for copy in loads():
        copy.wait()

    def up_copy(k):
        return remote(
            Q.at[k, :, pl.ds(top, SUB)], Q.at[k, :, pl.ds(top + rows, SUB)], hs.at[0, k], hr.at[0, k],
            {"tile": tile - 1},
        )

    def down_copy(k):
        return remote(
            Q.at[k, :, pl.ds(top + rows - SUB, SUB)], Q.at[k, :, pl.ds(top - SUB, SUB)], hs.at[1, k], hr.at[1, k],
            {"tile": tile + 1},
        )

    order = [n, n + 1] + list(range(n))
    for k in order:
        @pl.when(has_up)
        def _(k=k):
            up_copy(k).start()

        @pl.when(has_down)
        def _(k=k):
            down_copy(k).start()

    def halo_wait(k):
        @pl.when(has_down)
        def _():
            up_copy(k).wait_recv()

        @pl.when(has_up)
        def _():
            down_copy(k).wait_recv()

    blank = jnp.zeros((SUB, LANES), jnp.float32)

    @pl.when(jnp.logical_not(has_up))
    def _():
        for k in range(n + 2):
            for b in blocks:
                Q[k, b, pl.ds(top - SUB, SUB)] = blank
        for b in blocks:
            U0[b] = blank
            U1[b] = blank

    @pl.when(jnp.logical_not(has_down))
    def _():
        for k in range(n + 2):
            for b in blocks:
                Q[k, b, pl.ds(top + rows, SUB)] = blank
        for b in blocks:
            L0[b] = blank
            L1[b] = blank

    def spread_start(src, main, up, low, ssem, rsem, edges):
        for d in range(1, groups):
            remote(src, main.at[me], ssem.at[0, d], rsem.at[0, d], at(partner(d))).start()
        if edges:
            @pl.when(has_up)
            def _():
                for d in blocks:
                    remote(src.at[pl.ds(0, SUB)], low.at[me], ssem.at[1, d], rsem.at[1, d], at(partner(d), tile - 1)).start()

            @pl.when(has_down)
            def _():
                for d in blocks:
                    remote(src.at[pl.ds(rows - SUB, SUB)], up.at[me], ssem.at[2, d], rsem.at[2, d], at(partner(d), tile + 1)).start()

    def spread_recv(src, main, up, low, ssem, rsem, edges):
        for d in range(1, groups):
            remote(src, main.at[sender(d)], ssem.at[0, d], rsem.at[0, d], at(sender(d))).wait_recv()
        if edges:
            @pl.when(has_down)
            def _():
                for d in blocks:
                    remote(src.at[pl.ds(0, SUB)], low.at[sender(d)], ssem.at[1, d], rsem.at[1, d], at(sender(d))).wait_recv()

            @pl.when(has_up)
            def _():
                for d in blocks:
                    remote(src.at[pl.ds(0, SUB)], up.at[sender(d)], ssem.at[2, d], rsem.at[2, d], at(sender(d))).wait_recv()

    def spread_sent(src, main, up, low, ssem, rsem, edges):
        for d in range(1, groups):
            remote(src, main.at[me], ssem.at[0, d], rsem.at[0, d], at(partner(d))).wait_send()
        if edges:
            @pl.when(has_up)
            def _():
                for d in blocks:
                    remote(src.at[pl.ds(0, SUB)], low.at[me], ssem.at[1, d], rsem.at[1, d], at(partner(d), tile - 1)).wait_send()

            @pl.when(has_down)
            def _():
                for d in blocks:
                    remote(src.at[pl.ds(0, SUB)], up.at[me], ssem.at[2, d], rsem.at[2, d], at(partner(d), tile + 1)).wait_send()

    def deal(src, dst, ssem, rsem):
        return [
            remote(src.at[partner(d)], dst.at[me], ssem.at[0, d], rsem.at[0, d], at(partner(d)))
            for d in range(1, groups)
        ]

    def dealt_wait(src, dst, ssem, rsem):
        for d in range(1, groups):
            remote(src.at[0], dst.at[sender(d)], ssem.at[0, d], rsem.at[0, d], at(sender(d))).wait_recv()

    cell = cell_ref[0]
    w = weight_ref[0]
    wi = -w * innov_ref[0]
    count = cell.shape[1]
    row_of = cell // LANES
    col_of = cell % LANES
    pick_r = lax.broadcasted_iota(jnp.int32, (rows, count), 0) == row_of
    pick_c = (lax.broadcasted_iota(jnp.int32, (LANES, count), 0) == col_of).astype(jnp.float32)
    left = jnp.concatenate([jnp.where(pick_r, w, 0.0), jnp.where(pick_r, wi, 0.0)], axis=0)
    both = lax.dot_general(
        left, pick_c, (((1,), (1,)), ((), ())),
        precision=lax.Precision.HIGHEST, preferred_element_type=jnp.float32,
    )
    OBW[...] = both[:rows]
    OBI[...] = both[rows:]
    G0[...] = both[rows:]
    M0[me] = both[rows:]
    spread0 = (G0, M0, U0, L0, s0, r0, True)
    spread_start(*spread0)

    halo_wait(n)
    halo_wait(n + 1)

    def coefficients(i, carry):
        r = pl.ds(pl.multiple_of(top - SUB + i * SUB, SUB), SUB)
        for b in blocks:
            cx = Q[n, b, r]
            cy = Q[n + 1, b, r]
            C[0, b, r] = 1.0 - jnp.abs(cx) - jnp.abs(cy)
            C[1, b, r] = jnp.maximum(cx, 0.0)
            C[2, b, r] = -jnp.minimum(cx, 0.0)
            C[3, b, r] = jnp.maximum(cy, 0.0)
            C[4, b, r] = -jnp.minimum(cy, 0.0)
        return carry

    lax.fori_loop(0, rows // SUB + 2, coefficients, 0)
    for i in range(tall // SUB):
        for b in blocks:
            OWN[b, pl.ds(i * SUB, SUB)] = blank

    def advect(get, first, i):
        base = first + i * SUB
        q = [get(b, base) for b in blocks]
        before = moved(q, -1, lane)
        after = moved(q, 1, lane)
        out = []
        for b in blocks:
            r = pl.ds(base, SUB)
            out.append(
                (C[0, b, r] * q[b] + C[1, b, r] * get(b, base - 1))
                + (C[2, b, r] * get(b, base + 1) + C[3, b, r] * before[b])
                + C[4, b, r] * after[b]
            )
        return out

    def forecast(k, carry):
        halo_wait(k)
        for i in range(rows // SUB + 2):
            new = advect(lambda b, r: Q[k, b, pl.ds(r, SUB)], top - SUB, i)
            for b in blocks:
                T1[b, pl.ds(top - SUB + i * SUB, SUB)] = new[b]
        for i in range(rows // SUB + 2):
            new = advect(lambda b, r: T1[b, pl.ds(r, SUB)], top - SUB, i)
            for b in blocks:
                T2[b, pl.ds(top - SUB + i * SUB, SUB)] = new[b]
        for i in range(tall // SUB):
            new = advect(lambda b, r: T2[b, pl.ds(r, SUB)], top - REACH, i)
            r = pl.ds(i * SUB, SUB)
            for b in blocks:
                D[k, b, r] = new[b]
                OWN[b, r] += new[b] * (1.0 / n)
        return carry

    lax.fori_loop(0, n, forecast, 0)

    mean_out = deal(OWN, MR, sm1, rm1)
    for copy in mean_out:
        copy.start()
    MR[me] = OWN[me]

    def centre(k, carry):
        for i in range(tall // SUB):
            r = pl.ds(i * SUB, SUB)
            for b in blocks:
                D[k, b, r] = D[k, b, r] - OWN[b, r]
        return carry

    lax.fori_loop(0, n, centre, 0)

    entries = offs.shape[0]
    weights = [wts[s] for s in range(entries)]
    weight_sum = weights[0]
    for s in range(1, entries):
        weight_sum = weight_sum + weights[s]
    inverse = 1.0 / jnp.full((SUB, LANES), weight_sum, jnp.float32)
    scale = inverse * inverse * (-STEP_SIZE / (total - 1))
    first_row = tile * rows - RADIUS
    end_row = tiles * rows
    sub = lax.broadcasted_iota(jnp.int32, (SUB, LANES), 0)

    def assemble(main, up, low):
        for b in blocks:
            H[b, pl.ds(0, REACH)] = up[b, pl.ds(SUB - REACH, REACH)]
            H[b, pl.ds(REACH, rows)] = main[b]
            H[b, pl.ds(REACH + rows, REACH)] = low[b, pl.ds(0, REACH)]

    def clear():
        for i in range(rows // SUB):
            for b in blocks:
                ACC[b, pl.ds(i * SUB, SUB)] = blank

    def apply(k, carry):
        def lift(i, c1):
            r = pl.ds(pl.multiple_of(i * SUB, SUB), SUB)
            u = [D[k, b, r] * H[b, r] for b in blocks]
            for c in SHIFTS:
                v = moved(u, c, lane)
                for b in blocks:
                    U[c + RADIUS, b, r] = v[b]
            return c1

        lax.fori_loop(0, tall // SUB, lift, 0)

        def adjoint(i, c1):
            z = []
            place = first_row + i * SUB + sub
            keep = (place >= 0) & (place < end_row)
            for b in blocks:
                acc = None
                for s in range(entries):
                    part = weights[s] * U[RADIUS - offs[s, 1], b, pl.ds(i * SUB + RADIUS - offs[s, 0], SUB)]
                    acc = part if acc is None else acc + part
                z.append(jnp.where(keep, acc, 0.0))
            r = pl.ds(pl.multiple_of(i * SUB, SUB), SUB)
            for c in SHIFTS:
                v = moved(z, c, lane)
                for b in blocks:
                    Z[c + RADIUS, b, r] = v[b]
            return c1

        lax.fori_loop(0, tall // SUB, adjoint, 0)

        def direct(i, c1):
            r = pl.ds(pl.multiple_of(i * SUB, SUB), SUB)
            for b in blocks:
                acc = None
                for s in range(entries):
                    part = weights[s] * Z[RADIUS + offs[s, 1], b, pl.ds(i * SUB + RADIUS + offs[s, 0], SUB)]
                    acc = part if acc is None else acc + part
                ACC[b, r] += D[k, b, pl.ds(i * SUB + REACH, SUB)] * acc
            return c1

        lax.fori_loop(0, rows // SUB, direct, 0)
        return carry

    def publish(copies, dst):
        for i in range(rows // SUB):
            r = pl.ds(i * SUB, SUB)
            for b in blocks:
                XP[b, r] = ACC[b, r] * scale
        for copy in copies:
            copy.start()
        dst[me] = XP[me]

    spread_recv(*spread0)
    assemble(M0, U0, L0)
    clear()
    half = n // 2
    lax.fori_loop(0, half, apply, 0)
    dealt_wait(OWN, MR, sm1, rm1)
    mean = MR[0]
    for b in range(1, groups):
        mean = mean + MR[b]
    MB[...] = mean * (1.0 / groups)
    MG[me] = mean * (1.0 / groups)
    spread_mean = (MB, MG, None, None, sm2, rm2, False)
    spread_start(*spread_mean)
    lax.fori_loop(half, n, apply, 0)
    spread_recv(*spread_mean)
    for b in blocks:
        D[n, b] = (OWN[b] - MG[b]) * math.sqrt(n)
        D[n + 1, b] = jnp.full((tall, LANES), math.sqrt((total - 1) / groups), jnp.float32)
    lax.fori_loop(n, n + 2, apply, 0)
    first_out = deal(XP, R0, sx0, rx0)
    publish(first_out, R0)
    dealt_wait(XP, R0, sx0, rx0)
    x0 = R0[0]
    for b in range(1, groups):
        x0 = x0 + R0[b]
    X0[...] = x0 * (1.0 - STEP_SIZE)
    g1 = OBW[...] * x0 + OBI[...]
    G1[...] = g1
    M1[me] = g1
    spread1 = (G1, M1, U1, L1, s1, r1, True)
    spread_start(*spread1)
    for copy in first_out:
        copy.wait_send()
    spread_recv(*spread1)
    assemble(M1, U1, L1)
    clear()
    lax.fori_loop(0, n + 2, apply, 0)
    second_out = deal(XP, R1, sx1, rx1)
    publish(second_out, R1)
    dealt_wait(XP, R1, sx1, rx1)
    block = X0[...]
    for b in blocks:
        block = block + R1[b]
    NB[...] = block
    NM[me] = block
    inc_ref[...] = block
    spread_last = (NB, NM, None, None, sn, rn, False)
    spread_start(*spread_last)

    for k in order:
        @pl.when(has_up)
        def _(k=k):
            up_copy(k).wait_send()

        @pl.when(has_down)
        def _(k=k):
            down_copy(k).wait_send()

    spread_recv(*spread_last)
    writes = []
    for b in blocks:
        base = OWN[b, pl.ds(REACH, rows)] + NM[b]

        def finish(k, carry, b=b, base=base):
            Q[k, b, pl.ds(top, rows)] = D[k, b, pl.ds(REACH, rows)] + base
            return carry

        lax.fori_loop(0, n, finish, 0)
        copy = pltpu.make_async_copy(
            Q.at[pl.ds(0, n), b, pl.ds(top, rows)], out_hbm.at[:, :, pl.ds(b * LANES, LANES)], out_sem.at[b]
        )
        copy.start()
        writes.append(copy)
    spread_sent(*spread0)
    for copy in mean_out + second_out:
        copy.wait_send()
    spread_sent(*spread_mean)
    spread_sent(*spread1)
    spread_sent(*spread_last)
    for copy in writes:
        copy.wait()


def on_device(members, courant_x, courant_y, obs_cell, innovation, obs_weight, offsets, weights):
    n, rows, cols = members.shape
    groups = lax.axis_size(GROUP)
    n_grp = lax.axis_size("grp")
    assert cols == groups * LANES and rows % SUB == 0
    tall = rows + 2 * REACH
    deep = rows + 4 * SUB
    f32 = jnp.float32
    vmem = pltpu.VMEM
    dma = pltpu.SemaphoreType.DMA
    scratch = [
        vmem((n + 2, groups, deep, LANES), f32),
        vmem((5, groups, deep, LANES), f32),
        vmem((groups, deep, LANES), f32),
        vmem((groups, deep, LANES), f32),
        vmem((n + 2, groups, tall, LANES), f32),
        vmem((groups, tall, LANES), f32),
        vmem((groups, tall, LANES), f32),
        vmem((tall, LANES), f32),
        vmem((groups, tall, LANES), f32),
    ]
    scratch += [vmem((rows, LANES), f32)] * 4
    for _ in range(2):
        scratch += [vmem((groups, rows, LANES), f32), vmem((groups, SUB, LANES), f32), vmem((groups, SUB, LANES), f32)]
    scratch += [
        vmem((groups, tall, LANES), f32),
        vmem((len(SHIFTS), groups, tall + SUB, LANES), f32),
        vmem((len(SHIFTS), groups, tall, LANES), f32),
        vmem((groups, rows, LANES), f32),
        vmem((groups, rows, LANES), f32),
        vmem((rows, LANES), f32),
        vmem((groups, rows, LANES), f32),
        vmem((groups, rows, LANES), f32),
        vmem((rows, LANES), f32),
        vmem((groups, rows, LANES), f32),
        dma((3, groups)),
        dma((groups,)),
        dma((2, n + 2)),
        dma((2, n + 2)),
        dma((3, groups)),
        dma((3, groups)),
        dma((3, groups)),
        dma((3, groups)),
    ]
    scratch += [dma((1, groups))] * 10
    whole = pl.BlockSpec(memory_space=pltpu.VMEM)
    scalar = pl.BlockSpec(memory_space=pltpu.SMEM)
    left = pl.BlockSpec(memory_space=pl.ANY)
    return pl.pallas_call(
        functools.partial(kernel, (n, rows, groups, n_grp)),
        out_shape=(
            jax.ShapeDtypeStruct(members.shape, f32),
            jax.ShapeDtypeStruct((rows, LANES), f32),
        ),
        in_specs=[scalar, scalar, left, left, left, whole, whole, whole],
        out_specs=(left, whole),
        scratch_shapes=scratch,
        compiler_params=pltpu.CompilerParams(collective_id=0, has_side_effects=True, vmem_limit_bytes=40 << 20),
        name="cycle",
    )(offsets, weights, members, courant_x, courant_y, obs_cell, innovation, obs_weight)


def solution(mesh):
    placed = (
        P(GROUP, "tile", None),
        P("tile", None),
        P("tile", None),
        P("tile", GROUP, None),
        P("tile", GROUP, None),
        P("tile", GROUP, None),
        P(),
        P(),
    )
    return jax.shard_map(
        on_device,
        mesh=mesh,
        in_specs=placed,
        out_specs=(P(GROUP, "tile", None), P("tile", GROUP)),
        check_vma=False,
    )
```

```python
import functools
import math

import jax
import jax.numpy as jnp
from jax import lax
from jax.experimental import pallas as pl
from jax.experimental.pallas import tpu as pltpu
from jax.sharding import PartitionSpec as P

RADIUS = 2
FSTEPS = 3
STEP_SIZE = 0.25
GROUP = ("member", "grp")
MESH = pl.DeviceIdType.MESH
SUB = 8
LANES = 128
REACH = 2 * RADIUS
SHIFTS = tuple(range(-RADIUS, RADIUS + 1))


def remote(src, dst, send_sem, recv_sem, where):
    return pltpu.make_async_remote_copy(
        src_ref=src, dst_ref=dst, send_sem=send_sem, recv_sem=recv_sem, device_id=where, device_id_type=MESH
    )


def moved(blocks, c, lane):
    if c == 0:
        return blocks
    turned = [pltpu.roll(x, (-c) % LANES, 1) for x in blocks]
    nothing = jnp.zeros_like(blocks[0])
    out = []
    for b in range(len(blocks)):
        if c > 0:
            other = turned[b + 1] if b + 1 < len(blocks) else nothing
            out.append(jnp.where(lane >= LANES - c, other, turned[b]))
        else:
            other = turned[b - 1] if b > 0 else nothing
            out.append(jnp.where(lane < -c, other, turned[b]))
    return out


def kernel(
    shape,
    offs_hbm, wts_hbm, members, cx_hbm, cy_hbm, cell_hbm, innov_hbm, weight_hbm,
    out_hbm, inc_hbm,
    Q, C, T1, T2, D, OWN, MR, MB, MG, OBW, OBI, G0, G1,
    M0, U0, L0, M1, U1, L1, H, U, Z, ACC, XP, X0, R0, R1, NB, NM,
    offs, wts, cell_ref, innov_ref, weight_ref, inc_buf, small_sem,
    in_sem, out_sem, hs, hr, s0, r0, s1, r1, sm1, rm1, sm2, rm2, sx0, rx0, sx1, rx1, sn, rn,
):
    n, rows, groups, n_grp = shape
    total = n * groups
    tiles = lax.axis_size("tile")
    tile = lax.axis_index("tile")
    me = lax.axis_index("member") * n_grp + lax.axis_index("grp")
    has_up = tile > 0
    has_down = tile < tiles - 1
    top = 2 * SUB
    tall = rows + 2 * REACH
    lane = lax.broadcasted_iota(jnp.int32, (SUB, LANES), 1)
    blocks = range(groups)

    def at(p, t=None):
        where = {"member": p // n_grp, "grp": lax.rem(p, n_grp)}
        if t is not None:
            where["tile"] = t
        return where

    def partner(d):
        return lax.rem(me + d, groups)

    def sender(d):
        return lax.rem(me + groups - d, groups)

    def loads():
        for b in blocks:
            cols = pl.ds(b * LANES, LANES)
            yield pltpu.make_async_copy(cx_hbm.at[:, cols], Q.at[n, b, pl.ds(top, rows)], in_sem.at[1, b])
            yield pltpu.make_async_copy(cy_hbm.at[:, cols], Q.at[n + 1, b, pl.ds(top, rows)], in_sem.at[2, b])
        for b in blocks:
            cols = pl.ds(b * LANES, LANES)
            yield pltpu.make_async_copy(members.at[:, :, cols], Q.at[pl.ds(0, n), b, pl.ds(top, rows)], in_sem.at[0, b])

    small = [
        pltpu.make_async_copy(a, b, small_sem.at[i])
        for i, (a, b) in enumerate(
            [(cell_hbm, cell_ref), (innov_hbm, innov_ref), (weight_hbm, weight_ref), (offs_hbm, offs), (wts_hbm, wts)]
        )
    ]
    for copy in small:
        copy.start()
    for copy in loads():
        copy.start()

    barrier = pltpu.get_barrier_semaphore()
    for d in range(1, groups):
        pl.semaphore_signal(barrier, inc=1, device_id=at(partner(d)), device_id_type=MESH)

    @pl.when(has_up)
    def _():
        for d in blocks:
            pl.semaphore_signal(barrier, inc=1, device_id=at(partner(d), tile - 1), device_id_type=MESH)

    @pl.when(has_down)
    def _():
        for d in blocks:
            pl.semaphore_signal(barrier, inc=1, device_id=at(partner(d), tile + 1), device_id_type=MESH)

    sides = jnp.where(has_up, 1, 0) + jnp.where(has_down, 1, 0)
    for m in range(3):
        @pl.when(sides == m)
        def _(m=m):
            pl.semaphore_wait(barrier, groups - 1 + m * groups)

    for copy in loads():
        copy.wait()

    def up_copy(k):
        return remote(
            Q.at[k, :, pl.ds(top, SUB)], Q.at[k, :, pl.ds(top + rows, SUB)], hs.at[0, k], hr.at[0, k],
            {"tile": tile - 1},
        )

    def down_copy(k):
        return remote(
            Q.at[k, :, pl.ds(top + rows - SUB, SUB)], Q.at[k, :, pl.ds(top - SUB, SUB)], hs.at[1, k], hr.at[1, k],
            {"tile": tile + 1},
        )

    order = [n, n + 1] + list(range(n))
    for k in order:
        @pl.when(has_up)
        def _(k=k):
            up_copy(k).start()

        @pl.when(has_down)
        def _(k=k):
            down_copy(k).start()

    def halo_wait(k):
        @pl.when(has_down)
        def _():
            up_copy(k).wait_recv()

        @pl.when(has_up)
        def _():
            down_copy(k).wait_recv()

    blank = jnp.zeros((SUB, LANES), jnp.float32)

    @pl.when(jnp.logical_not(has_up))
    def _():
        for k in range(n + 2):
            for b in blocks:
                Q[k, b, pl.ds(top - SUB, SUB)] = blank
        for b in blocks:
            U0[b] = blank
            U1[b] = blank

    @pl.when(jnp.logical_not(has_down))
    def _():
        for k in range(n + 2):
            for b in blocks:
                Q[k, b, pl.ds(top + rows, SUB)] = blank
        for b in blocks:
            L0[b] = blank
            L1[b] = blank

    def spread_start(src, main, up, low, ssem, rsem, edges):
        for d in range(1, groups):
            remote(src, main.at[me], ssem.at[0, d], rsem.at[0, d], at(partner(d))).start()
        if edges:
            @pl.when(has_up)
            def _():
                for d in blocks:
                    remote(src.at[pl.ds(0, SUB)], low.at[me], ssem.at[1, d], rsem.at[1, d], at(partner(d), tile - 1)).start()

            @pl.when(has_down)
            def _():
                for d in blocks:
                    remote(src.at[pl.ds(rows - SUB, SUB)], up.at[me], ssem.at[2, d], rsem.at[2, d], at(partner(d), tile + 1)).start()

    def spread_recv(src, main, up, low, ssem, rsem, edges):
        for d in range(1, groups):
            remote(src, main.at[sender(d)], ssem.at[0, d], rsem.at[0, d], at(sender(d))).wait_recv()
        if edges:
            @pl.when(has_down)
            def _():
                for d in blocks:
                    remote(src.at[pl.ds(0, SUB)], low.at[sender(d)], ssem.at[1, d], rsem.at[1, d], at(sender(d))).wait_recv()

            @pl.when(has_up)
            def _():
                for d in blocks:
                    remote(src.at[pl.ds(0, SUB)], up.at[sender(d)], ssem.at[2, d], rsem.at[2, d], at(sender(d))).wait_recv()

    def spread_sent(src, main, up, low, ssem, rsem, edges):
        for d in range(1, groups):
            remote(src, main.at[me], ssem.at[0, d], rsem.at[0, d], at(partner(d))).wait_send()
        if edges:
            @pl.when(has_up)
            def _():
                for d in blocks:
                    remote(src.at[pl.ds(0, SUB)], low.at[me], ssem.at[1, d], rsem.at[1, d], at(partner(d), tile - 1)).wait_send()

            @pl.when(has_down)
            def _():
                for d in blocks:
                    remote(src.at[pl.ds(0, SUB)], up.at[me], ssem.at[2, d], rsem.at[2, d], at(partner(d), tile + 1)).wait_send()

    def deal(src, dst, ssem, rsem):
        return [
            remote(src.at[partner(d)], dst.at[me], ssem.at[0, d], rsem.at[0, d], at(partner(d)))
            for d in range(1, groups)
        ]

    def dealt_wait(src, dst, ssem, rsem):
        for d in range(1, groups):
            remote(src.at[0], dst.at[sender(d)], ssem.at[0, d], rsem.at[0, d], at(sender(d))).wait_recv()

    for copy in small:
        copy.wait()

    cell = cell_ref[0]
    w = weight_ref[0]
    wi = -w * innov_ref[0]
    count = cell.shape[1]
    row_of = cell // LANES
    col_of = cell % LANES
    pick_r = lax.broadcasted_iota(jnp.int32, (rows, count), 0) == row_of
    pick_c = (lax.broadcasted_iota(jnp.int32, (LANES, count), 0) == col_of).astype(jnp.float32)
    left = jnp.concatenate([jnp.where(pick_r, w, 0.0), jnp.where(pick_r, wi, 0.0)], axis=0)
    both = lax.dot_general(
        left, pick_c, (((1,), (1,)), ((), ())),
        precision=lax.Precision.HIGHEST, preferred_element_type=jnp.float32,
    )
    OBW[...] = both[:rows]
    OBI[...] = both[rows:]
    G0[...] = both[rows:]
    M0[me] = both[rows:]
    spread0 = (G0, M0, U0, L0, s0, r0, True)
    spread_start(*spread0)

    halo_wait(n)
    halo_wait(n + 1)

    def coefficients(i, carry):
        r = pl.ds(pl.multiple_of(top - SUB + i * SUB, SUB), SUB)
        for b in blocks:
            cx = Q[n, b, r]
            cy = Q[n + 1, b, r]
            C[0, b, r] = 1.0 - jnp.abs(cx) - jnp.abs(cy)
            C[1, b, r] = jnp.maximum(cx, 0.0)
            C[2, b, r] = -jnp.minimum(cx, 0.0)
            C[3, b, r] = jnp.maximum(cy, 0.0)
            C[4, b, r] = -jnp.minimum(cy, 0.0)
        return carry

    lax.fori_loop(0, rows // SUB + 2, coefficients, 0)
    for i in range(tall // SUB):
        for b in blocks:
            OWN[b, pl.ds(i * SUB, SUB)] = blank

    def advect(get, first, i):
        base = first + i * SUB
        q = [get(b, base) for b in blocks]
        before = moved(q, -1, lane)
        after = moved(q, 1, lane)
        out = []
        for b in blocks:
            r = pl.ds(base, SUB)
            out.append(
                (C[0, b, r] * q[b] + C[1, b, r] * get(b, base - 1))
                + (C[2, b, r] * get(b, base + 1) + C[3, b, r] * before[b])
                + C[4, b, r] * after[b]
            )
        return out

    def forecast(k, carry):
        halo_wait(k)
        for i in range(rows // SUB + 2):
            new = advect(lambda b, r: Q[k, b, pl.ds(r, SUB)], top - SUB, i)
            for b in blocks:
                T1[b, pl.ds(top - SUB + i * SUB, SUB)] = new[b]
        for i in range(rows // SUB + 2):
            new = advect(lambda b, r: T1[b, pl.ds(r, SUB)], top - SUB, i)
            for b in blocks:
                T2[b, pl.ds(top - SUB + i * SUB, SUB)] = new[b]
        for i in range(tall // SUB):
            new = advect(lambda b, r: T2[b, pl.ds(r, SUB)], top - REACH, i)
            r = pl.ds(i * SUB, SUB)
            for b in blocks:
                D[k, b, r] = new[b]
                OWN[b, r] += new[b] * (1.0 / n)
        return carry

    lax.fori_loop(0, n, forecast, 0)

    mean_out = deal(OWN, MR, sm1, rm1)
    for copy in mean_out:
        copy.start()
    MR[me] = OWN[me]

    def centre(k, carry):
        for i in range(tall // SUB):
            r = pl.ds(i * SUB, SUB)
            for b in blocks:
                D[k, b, r] = D[k, b, r] - OWN[b, r]
        return carry

    lax.fori_loop(0, n, centre, 0)

    entries = offs.shape[1]
    weights = [wts[s] for s in range(entries)]
    weight_sum = weights[0]
    for s in range(1, entries):
        weight_sum = weight_sum + weights[s]
    inverse = 1.0 / jnp.full((SUB, LANES), weight_sum, jnp.float32)
    scale = inverse * inverse * (-STEP_SIZE / (total - 1))
    first_row = tile * rows - RADIUS
    end_row = tiles * rows
    sub = lax.broadcasted_iota(jnp.int32, (SUB, LANES), 0)

    def assemble(main, up, low):
        for b in blocks:
            H[b, pl.ds(0, REACH)] = up[b, pl.ds(SUB - REACH, REACH)]
            H[b, pl.ds(REACH, rows)] = main[b]
            H[b, pl.ds(REACH + rows, REACH)] = low[b, pl.ds(0, REACH)]

    def clear():
        for i in range(rows // SUB):
            for b in blocks:
                ACC[b, pl.ds(i * SUB, SUB)] = blank

    def apply(k, carry):
        def lift(i, c1):
            r = pl.ds(pl.multiple_of(i * SUB, SUB), SUB)
            u = [D[k, b, r] * H[b, r] for b in blocks]
            for c in SHIFTS:
                v = moved(u, c, lane)
                for b in blocks:
                    U[c + RADIUS, b, r] = v[b]
            return c1

        lax.fori_loop(0, tall // SUB, lift, 0, unroll=True)

        def adjoint(i, c1):
            z = []
            place = first_row + i * SUB + sub
            keep = (place >= 0) & (place < end_row)
            for b in blocks:
                acc = None
                for s in range(entries):
                    part = weights[s] * U[RADIUS - offs[1, s], b, pl.ds(i * SUB + RADIUS - offs[0, s], SUB)]
                    acc = part if acc is None else acc + part
                z.append(jnp.where(keep, acc, 0.0))
            r = pl.ds(pl.multiple_of(i * SUB, SUB), SUB)
            for c in SHIFTS:
                v = moved(z, c, lane)
                for b in blocks:
                    Z[c + RADIUS, b, r] = v[b]
            return c1

        lax.fori_loop(0, tall // SUB, adjoint, 0, unroll=True)

        def direct(i, c1):
            r = pl.ds(pl.multiple_of(i * SUB, SUB), SUB)
            for b in blocks:
                acc = None
                for s in range(entries):
                    part = weights[s] * Z[RADIUS + offs[1, s], b, pl.ds(i * SUB + RADIUS + offs[0, s], SUB)]
                    acc = part if acc is None else acc + part
                ACC[b, r] += D[k, b, pl.ds(i * SUB + REACH, SUB)] * acc
            return c1

        lax.fori_loop(0, rows // SUB, direct, 0, unroll=True)
        return carry

    def publish(copies, dst):
        for i in range(rows // SUB):
            r = pl.ds(i * SUB, SUB)
            for b in blocks:
                XP[b, r] = ACC[b, r] * scale
        for copy in copies:
            copy.start()
        dst[me] = XP[me]

    spread_recv(*spread0)
    assemble(M0, U0, L0)
    clear()
    half = n // 2
    lax.fori_loop(0, half, apply, 0)
    dealt_wait(OWN, MR, sm1, rm1)
    mean = MR[0]
    for b in range(1, groups):
        mean = mean + MR[b]
    MB[...] = mean * (1.0 / groups)
    MG[me] = mean * (1.0 / groups)
    spread_mean = (MB, MG, None, None, sm2, rm2, False)
    spread_start(*spread_mean)
    lax.fori_loop(half, n, apply, 0)
    spread_recv(*spread_mean)
    for b in blocks:
        D[n, b] = (OWN[b] - MG[b]) * math.sqrt(n)
        D[n + 1, b] = jnp.full((tall, LANES), math.sqrt((total - 1) / groups), jnp.float32)
    lax.fori_loop(n, n + 2, apply, 0)
    first_out = deal(XP, R0, sx0, rx0)
    publish(first_out, R0)
    dealt_wait(XP, R0, sx0, rx0)
    x0 = R0[0]
    for b in range(1, groups):
        x0 = x0 + R0[b]
    X0[...] = x0 * (1.0 - STEP_SIZE)
    g1 = OBW[...] * x0 + OBI[...]
    G1[...] = g1
    M1[me] = g1
    spread1 = (G1, M1, U1, L1, s1, r1, True)
    spread_start(*spread1)
    for copy in first_out:
        copy.wait_send()
    spread_recv(*spread1)
    assemble(M1, U1, L1)
    clear()
    lax.fori_loop(0, n + 2, apply, 0)
    second_out = deal(XP, R1, sx1, rx1)
    publish(second_out, R1)
    dealt_wait(XP, R1, sx1, rx1)
    block = X0[...]
    for b in blocks:
        block = block + R1[b]
    NB[...] = block
    NM[me] = block
    inc_buf[...] = block
    inc_copy = pltpu.make_async_copy(inc_buf, inc_hbm, small_sem.at[5])
    inc_copy.start()
    spread_last = (NB, NM, None, None, sn, rn, False)
    spread_start(*spread_last)

    for k in order:
        @pl.when(has_up)
        def _(k=k):
            up_copy(k).wait_send()

        @pl.when(has_down)
        def _(k=k):
            down_copy(k).wait_send()

    spread_recv(*spread_last)
    writes = []
    for b in blocks:
        base = OWN[b, pl.ds(REACH, rows)] + NM[b]

        def finish(k, carry, b=b, base=base):
            Q[k, b, pl.ds(top, rows)] = D[k, b, pl.ds(REACH, rows)] + base
            return carry

        lax.fori_loop(0, n, finish, 0)
        copy = pltpu.make_async_copy(
            Q.at[pl.ds(0, n), b, pl.ds(top, rows)], out_hbm.at[:, :, pl.ds(b * LANES, LANES)], out_sem.at[b]
        )
        copy.start()
        writes.append(copy)
    spread_sent(*spread0)
    for copy in mean_out + second_out:
        copy.wait_send()
    spread_sent(*spread_mean)
    spread_sent(*spread1)
    spread_sent(*spread_last)
    for copy in writes:
        copy.wait()
    inc_copy.wait()


def on_device(members, courant_x, courant_y, obs_cell, innovation, obs_weight, offsets, weights):
    n, rows, cols = members.shape
    groups = lax.axis_size(GROUP)
    n_grp = lax.axis_size("grp")
    assert cols == groups * LANES and rows % SUB == 0
    tall = rows + 2 * REACH
    deep = rows + 4 * SUB
    f32 = jnp.float32
    vmem = pltpu.VMEM
    dma = pltpu.SemaphoreType.DMA
    scratch = [
        vmem((n + 2, groups, deep, LANES), f32),
        vmem((5, groups, deep, LANES), f32),
        vmem((groups, deep, LANES), f32),
        vmem((groups, deep, LANES), f32),
        vmem((n + 2, groups, tall, LANES), f32),
        vmem((groups, tall, LANES), f32),
        vmem((groups, tall, LANES), f32),
        vmem((tall, LANES), f32),
        vmem((groups, tall, LANES), f32),
    ]
    scratch += [vmem((rows, LANES), f32)] * 4
    for _ in range(2):
        scratch += [vmem((groups, rows, LANES), f32), vmem((groups, SUB, LANES), f32), vmem((groups, SUB, LANES), f32)]
    scratch += [
        vmem((groups, tall, LANES), f32),
        vmem((len(SHIFTS), groups, tall + SUB, LANES), f32),
        vmem((len(SHIFTS), groups, tall, LANES), f32),
        vmem((groups, rows, LANES), f32),
        vmem((groups, rows, LANES), f32),
        vmem((rows, LANES), f32),
        vmem((groups, rows, LANES), f32),
        vmem((groups, rows, LANES), f32),
        vmem((rows, LANES), f32),
        vmem((groups, rows, LANES), f32),
        pltpu.SMEM((2, offsets.shape[0]), jnp.int32),
        pltpu.SMEM(weights.shape, f32),
        vmem(obs_cell.shape, jnp.int32),
        vmem(innovation.shape, f32),
        vmem(obs_weight.shape, f32),
        vmem((rows, LANES), f32),
        dma((6,)),
        dma((3, groups)),
        dma((groups,)),
        dma((2, n + 2)),
        dma((2, n + 2)),
        dma((3, groups)),
        dma((3, groups)),
        dma((3, groups)),
        dma((3, groups)),
    ]
    scratch += [dma((1, groups))] * 10
    left = pl.BlockSpec(memory_space=pltpu.HBM)
    return pl.pallas_call(
        functools.partial(kernel, (n, rows, groups, n_grp)),
        out_shape=(
            jax.ShapeDtypeStruct(members.shape, f32),
            jax.ShapeDtypeStruct((rows, LANES), f32),
        ),
        in_specs=[left] * 8,
        out_specs=(left, left),
        scratch_shapes=scratch,
        compiler_params=pltpu.CompilerParams(collective_id=0, has_side_effects=True, vmem_limit_bytes=67043328),
        name="cycle",
    )(offsets.T, weights, members, courant_x, courant_y, obs_cell, innovation, obs_weight)


def solution(mesh):
    placed = (
        P(GROUP, "tile", None),
        P("tile", None),
        P("tile", None),
        P("tile", GROUP, None),
        P("tile", GROUP, None),
        P("tile", GROUP, None),
        P(),
        P(),
    )
    return jax.shard_map(
        on_device,
        mesh=mesh,
        in_specs=placed,
        out_specs=(P(GROUP, "tile", None), P("tile", GROUP)),
        check_vma=False,
    )
```

```python
import functools
import math

import jax
import jax.numpy as jnp
from jax import lax
from jax.experimental import pallas as pl
from jax.experimental.pallas import tpu as pltpu
from jax.sharding import PartitionSpec as P

RADIUS = 2
FSTEPS = 3
STEP_SIZE = 0.25
GROUP = ("member", "grp")
MESH = pl.DeviceIdType.MESH
SUB = 8
LANES = 128
REACH = 2 * RADIUS
SHIFTS = tuple(range(-RADIUS, RADIUS + 1))


def remote(src, dst, send_sem, recv_sem, where):
    return pltpu.make_async_remote_copy(
        src_ref=src, dst_ref=dst, send_sem=send_sem, recv_sem=recv_sem, device_id=where, device_id_type=MESH
    )


def moved(blocks, c, lane):
    if c == 0:
        return blocks
    turned = [pltpu.roll(x, (-c) % LANES, 1) for x in blocks]
    nothing = jnp.zeros_like(blocks[0])
    out = []
    for b in range(len(blocks)):
        if c > 0:
            other = turned[b + 1] if b + 1 < len(blocks) else nothing
            out.append(jnp.where(lane >= LANES - c, other, turned[b]))
        else:
            other = turned[b - 1] if b > 0 else nothing
            out.append(jnp.where(lane < -c, other, turned[b]))
    return out


def kernel(
    shape,
    offs_hbm, wts_hbm, members, cx_hbm, cy_hbm, cell_hbm, innov_hbm, weight_hbm,
    out_hbm, inc_hbm, full_hbm,
    Q, C, T1, T2, D, OWN, MR, MB, MG, OBW, OBI, G0, G1,
    M0, U0, L0, M1, U1, L1, H, U, Z, ACC, XP, X0, R0, R1, NB, NM,
    offs, wts, cell_ref, innov_ref, weight_ref, inc_buf, small_sem,
    F, full_sem,
    in_sem, out_sem, hs, hr, s0, r0, s1, r1, sm1, rm1, sm2, rm2, sx0, rx0, sx1, rx1, sn, rn,
):
    n, rows, groups, n_grp = shape
    total = n * groups
    tiles = lax.axis_size("tile")
    tile = lax.axis_index("tile")
    me = lax.axis_index("member") * n_grp + lax.axis_index("grp")
    has_up = tile > 0
    has_down = tile < tiles - 1
    top = 2 * SUB
    tall = rows + 2 * REACH
    lane = lax.broadcasted_iota(jnp.int32, (SUB, LANES), 1)
    blocks = range(groups)

    def at(p, t=None):
        where = {"member": p // n_grp, "grp": lax.rem(p, n_grp)}
        if t is not None:
            where["tile"] = t
        return where

    def partner(d):
        return lax.rem(me + d, groups)

    def sender(d):
        return lax.rem(me + groups - d, groups)

    def loads():
        for b in blocks:
            cols = pl.ds(b * LANES, LANES)
            yield pltpu.make_async_copy(cx_hbm.at[:, cols], Q.at[n, b, pl.ds(top, rows)], in_sem.at[1, b])
            yield pltpu.make_async_copy(cy_hbm.at[:, cols], Q.at[n + 1, b, pl.ds(top, rows)], in_sem.at[2, b])
        for b in blocks:
            cols = pl.ds(b * LANES, LANES)
            yield pltpu.make_async_copy(members.at[:, :, cols], Q.at[pl.ds(0, n), b, pl.ds(top, rows)], in_sem.at[0, b])

    small = [
        pltpu.make_async_copy(a, b, small_sem.at[i])
        for i, (a, b) in enumerate(
            [(cell_hbm, cell_ref), (innov_hbm, innov_ref), (weight_hbm, weight_ref), (offs_hbm, offs), (wts_hbm, wts)]
        )
    ]
    for copy in small:
        copy.start()
    for copy in loads():
        copy.start()

    barrier = pltpu.get_barrier_semaphore()
    for d in range(1, groups):
        pl.semaphore_signal(barrier, inc=1, device_id=at(partner(d)), device_id_type=MESH)

    @pl.when(has_up)
    def _():
        for d in blocks:
            pl.semaphore_signal(barrier, inc=1, device_id=at(partner(d), tile - 1), device_id_type=MESH)

    @pl.when(has_down)
    def _():
        for d in blocks:
            pl.semaphore_signal(barrier, inc=1, device_id=at(partner(d), tile + 1), device_id_type=MESH)

    for copy in small:
        copy.wait()

    cell = cell_ref[0]
    w = weight_ref[0]
    wi = -w * innov_ref[0]
    count = cell.shape[1]
    row_of = cell // LANES
    col_of = cell % LANES
    pick_r = lax.broadcasted_iota(jnp.int32, (rows, count), 0) == row_of
    pick_c = (lax.broadcasted_iota(jnp.int32, (LANES, count), 0) == col_of).astype(jnp.float32)
    left = jnp.concatenate([jnp.where(pick_r, w, 0.0), jnp.where(pick_r, wi, 0.0)], axis=0)
    both = lax.dot_general(
        left, pick_c, (((1,), (1,)), ((), ())),
        precision=lax.Precision.HIGHEST, preferred_element_type=jnp.float32,
    )
    OBW[...] = both[:rows]
    OBI[...] = both[rows:]
    G0[...] = both[rows:]
    M0[me] = both[rows:]

    sides = jnp.where(has_up, 1, 0) + jnp.where(has_down, 1, 0)
    for m in range(3):
        @pl.when(sides == m)
        def _(m=m):
            pl.semaphore_wait(barrier, groups - 1 + m * groups)


    def up_copy(k):
        return remote(
            Q.at[k, :, pl.ds(top, SUB)], Q.at[k, :, pl.ds(top + rows, SUB)], hs.at[0, k], hr.at[0, k],
            {"tile": tile - 1},
        )

    def down_copy(k):
        return remote(
            Q.at[k, :, pl.ds(top + rows - SUB, SUB)], Q.at[k, :, pl.ds(top - SUB, SUB)], hs.at[1, k], hr.at[1, k],
            {"tile": tile + 1},
        )

    def halo_wait(k):
        @pl.when(has_down)
        def _():
            up_copy(k).wait_recv()

        @pl.when(has_up)
        def _():
            down_copy(k).wait_recv()

    blank = jnp.zeros((SUB, LANES), jnp.float32)

    @pl.when(jnp.logical_not(has_up))
    def _():
        for k in range(n + 2):
            for b in blocks:
                Q[k, b, pl.ds(top - SUB, SUB)] = blank
        for b in blocks:
            U0[b] = blank
            U1[b] = blank

    @pl.when(jnp.logical_not(has_down))
    def _():
        for k in range(n + 2):
            for b in blocks:
                Q[k, b, pl.ds(top + rows, SUB)] = blank
        for b in blocks:
            L0[b] = blank
            L1[b] = blank

    def spread_start(src, main, up, low, ssem, rsem, edges):
        for d in range(1, groups):
            remote(src, main.at[me], ssem.at[0, d], rsem.at[0, d], at(partner(d))).start()
        if edges:
            @pl.when(has_up)
            def _():
                for d in blocks:
                    remote(src.at[pl.ds(0, SUB)], low.at[me], ssem.at[1, d], rsem.at[1, d], at(partner(d), tile - 1)).start()

            @pl.when(has_down)
            def _():
                for d in blocks:
                    remote(src.at[pl.ds(rows - SUB, SUB)], up.at[me], ssem.at[2, d], rsem.at[2, d], at(partner(d), tile + 1)).start()

    def spread_recv(src, main, up, low, ssem, rsem, edges):
        for d in range(1, groups):
            remote(src, main.at[sender(d)], ssem.at[0, d], rsem.at[0, d], at(sender(d))).wait_recv()
        if edges:
            @pl.when(has_down)
            def _():
                for d in blocks:
                    remote(src.at[pl.ds(0, SUB)], low.at[sender(d)], ssem.at[1, d], rsem.at[1, d], at(sender(d))).wait_recv()

            @pl.when(has_up)
            def _():
                for d in blocks:
                    remote(src.at[pl.ds(0, SUB)], up.at[sender(d)], ssem.at[2, d], rsem.at[2, d], at(sender(d))).wait_recv()

    def spread_sent(src, main, up, low, ssem, rsem, edges):
        for d in range(1, groups):
            remote(src, main.at[me], ssem.at[0, d], rsem.at[0, d], at(partner(d))).wait_send()
        if edges:
            @pl.when(has_up)
            def _():
                for d in blocks:
                    remote(src.at[pl.ds(0, SUB)], low.at[me], ssem.at[1, d], rsem.at[1, d], at(partner(d), tile - 1)).wait_send()

            @pl.when(has_down)
            def _():
                for d in blocks:
                    remote(src.at[pl.ds(0, SUB)], up.at[me], ssem.at[2, d], rsem.at[2, d], at(partner(d), tile + 1)).wait_send()

    def deal(src, dst, ssem, rsem):
        return [
            remote(src.at[partner(d)], dst.at[me], ssem.at[0, d], rsem.at[0, d], at(partner(d)))
            for d in range(1, groups)
        ]

    def dealt_wait(src, dst, ssem, rsem):
        for d in range(1, groups):
            remote(src.at[0], dst.at[sender(d)], ssem.at[0, d], rsem.at[0, d], at(sender(d))).wait_recv()

    spread0 = (G0, M0, U0, L0, s0, r0, True)
    spread_start(*spread0)
    for copy in loads():
        copy.wait()

    order = [n, n + 1] + list(range(n))
    for k in order:
        @pl.when(has_up)
        def _(k=k):
            up_copy(k).start()

        @pl.when(has_down)
        def _(k=k):
            down_copy(k).start()


    halo_wait(n)
    halo_wait(n + 1)

    def coefficients(i, carry):
        r = pl.ds(pl.multiple_of(top - SUB + i * SUB, SUB), SUB)
        for b in blocks:
            cx = Q[n, b, r]
            cy = Q[n + 1, b, r]
            C[0, b, r] = 1.0 - jnp.abs(cx) - jnp.abs(cy)
            C[1, b, r] = jnp.maximum(cx, 0.0)
            C[2, b, r] = -jnp.minimum(cx, 0.0)
            C[3, b, r] = jnp.maximum(cy, 0.0)
            C[4, b, r] = -jnp.minimum(cy, 0.0)
        return carry

    lax.fori_loop(0, rows // SUB + 2, coefficients, 0)
    for i in range(tall // SUB):
        for b in blocks:
            OWN[b, pl.ds(i * SUB, SUB)] = blank

    def advect(get, first, i):
        base = first + i * SUB
        q = [get(b, base) for b in blocks]
        before = moved(q, -1, lane)
        after = moved(q, 1, lane)
        out = []
        for b in blocks:
            r = pl.ds(base, SUB)
            out.append(
                (C[0, b, r] * q[b] + C[1, b, r] * get(b, base - 1))
                + (C[2, b, r] * get(b, base + 1) + C[3, b, r] * before[b])
                + C[4, b, r] * after[b]
            )
        return out

    def forecast(k, carry):
        halo_wait(k)
        for i in range(rows // SUB + 2):
            new = advect(lambda b, r: Q[k, b, pl.ds(r, SUB)], top - SUB, i)
            for b in blocks:
                T1[b, pl.ds(top - SUB + i * SUB, SUB)] = new[b]
        for i in range(rows // SUB + 2):
            new = advect(lambda b, r: T1[b, pl.ds(r, SUB)], top - SUB, i)
            for b in blocks:
                T2[b, pl.ds(top - SUB + i * SUB, SUB)] = new[b]
        for i in range(tall // SUB):
            new = advect(lambda b, r: T2[b, pl.ds(r, SUB)], top - REACH, i)
            r = pl.ds(i * SUB, SUB)
            for b in blocks:
                D[k, b, r] = new[b]
                OWN[b, r] += new[b] * (1.0 / n)
        for b in blocks:
            F[k, b] = D[k, b, pl.ds(REACH, rows)]
        return carry

    lax.fori_loop(0, n, forecast, 0)
    writes = [
        pltpu.make_async_copy(F.at[:, b], out_hbm.at[:, :, pl.ds(b * LANES, LANES)], out_sem.at[b]) for b in blocks
    ]
    for copy in writes:
        copy.start()

    mean_out = deal(OWN, MR, sm1, rm1)
    for copy in mean_out:
        copy.start()
    MR[me] = OWN[me]

    def centre(k, carry):
        for i in range(tall // SUB):
            r = pl.ds(i * SUB, SUB)
            for b in blocks:
                D[k, b, r] = D[k, b, r] - OWN[b, r]
        return carry

    lax.fori_loop(0, n, centre, 0)

    entries = offs.shape[1]
    weights = [wts[s] for s in range(entries)]
    weight_sum = weights[0]
    for s in range(1, entries):
        weight_sum = weight_sum + weights[s]
    inverse = 1.0 / jnp.full((SUB, LANES), weight_sum, jnp.float32)
    scale = inverse * inverse * (-STEP_SIZE / (total - 1))
    first_row = tile * rows - RADIUS
    end_row = tiles * rows
    sub = lax.broadcasted_iota(jnp.int32, (SUB, LANES), 0)

    def assemble(main, up, low):
        for b in blocks:
            H[b, pl.ds(0, REACH)] = up[b, pl.ds(SUB - REACH, REACH)]
            H[b, pl.ds(REACH, rows)] = main[b]
            H[b, pl.ds(REACH + rows, REACH)] = low[b, pl.ds(0, REACH)]

    def clear():
        for i in range(rows // SUB):
            for b in blocks:
                ACC[b, pl.ds(i * SUB, SUB)] = blank

    def apply(k, carry):
        def lift(i, c1):
            r = pl.ds(pl.multiple_of(i * SUB, SUB), SUB)
            u = [D[k, b, r] * H[b, r] for b in blocks]
            for c in SHIFTS:
                v = moved(u, c, lane)
                for b in blocks:
                    U[c + RADIUS, b, r] = v[b]
            return c1

        lax.fori_loop(0, tall // SUB, lift, 0, unroll=True)

        def adjoint(i, c1):
            z = []
            place = first_row + i * SUB + sub
            keep = (place >= 0) & (place < end_row)
            for b in blocks:
                acc = None
                for s in range(entries):
                    part = weights[s] * U[RADIUS - offs[1, s], b, pl.ds(i * SUB + RADIUS - offs[0, s], SUB)]
                    acc = part if acc is None else acc + part
                z.append(jnp.where(keep, acc, 0.0))
            r = pl.ds(pl.multiple_of(i * SUB, SUB), SUB)
            for c in SHIFTS:
                v = moved(z, c, lane)
                for b in blocks:
                    Z[c + RADIUS, b, r] = v[b]
            return c1

        lax.fori_loop(0, tall // SUB, adjoint, 0, unroll=True)

        def direct(i, c1):
            r = pl.ds(pl.multiple_of(i * SUB, SUB), SUB)
            for b in blocks:
                acc = None
                for s in range(entries):
                    part = weights[s] * Z[RADIUS + offs[1, s], b, pl.ds(i * SUB + RADIUS + offs[0, s], SUB)]
                    acc = part if acc is None else acc + part
                ACC[b, r] += D[k, b, pl.ds(i * SUB + REACH, SUB)] * acc
            return c1

        lax.fori_loop(0, rows // SUB, direct, 0, unroll=True)
        return carry

    def publish(copies, dst):
        for i in range(rows // SUB):
            r = pl.ds(i * SUB, SUB)
            for b in blocks:
                XP[b, r] = ACC[b, r] * scale
        for copy in copies:
            copy.start()
        dst[me] = XP[me]

    spread_recv(*spread0)
    assemble(M0, U0, L0)
    clear()
    half = n // 2
    lax.fori_loop(0, half, apply, 0)
    dealt_wait(OWN, MR, sm1, rm1)
    mean = MR[0]
    for b in range(1, groups):
        mean = mean + MR[b]
    MB[...] = mean * (1.0 / groups)
    MG[me] = mean * (1.0 / groups)
    spread_mean = (MB, MG, None, None, sm2, rm2, False)
    spread_start(*spread_mean)
    lax.fori_loop(half, n, apply, 0)
    spread_recv(*spread_mean)
    for b in blocks:
        D[n, b] = (OWN[b] - MG[b]) * math.sqrt(n)
        D[n + 1, b] = jnp.full((tall, LANES), math.sqrt((total - 1) / groups), jnp.float32)
    lax.fori_loop(n, n + 2, apply, 0)
    first_out = deal(XP, R0, sx0, rx0)
    publish(first_out, R0)
    dealt_wait(XP, R0, sx0, rx0)
    x0 = R0[0]
    for b in range(1, groups):
        x0 = x0 + R0[b]
    X0[...] = x0 * (1.0 - STEP_SIZE)
    g1 = OBW[...] * x0 + OBI[...]
    G1[...] = g1
    M1[me] = g1
    spread1 = (G1, M1, U1, L1, s1, r1, True)
    spread_start(*spread1)
    for copy in first_out:
        copy.wait_send()
    spread_recv(*spread1)
    assemble(M1, U1, L1)
    clear()
    lax.fori_loop(0, n + 2, apply, 0)
    second_out = deal(XP, R1, sx1, rx1)
    publish(second_out, R1)
    dealt_wait(XP, R1, sx1, rx1)
    block = X0[...]
    for b in blocks:
        block = block + R1[b]
    NB[...] = block
    NM[me] = block
    inc_buf[...] = block
    inc_copy = pltpu.make_async_copy(inc_buf, inc_hbm, small_sem.at[5])
    inc_copy.start()
    spread_last = (NB, NM, None, None, sn, rn, False)
    spread_start(*spread_last)

    for k in order:
        @pl.when(has_up)
        def _(k=k):
            up_copy(k).wait_send()

        @pl.when(has_down)
        def _(k=k):
            down_copy(k).wait_send()

    spread_recv(*spread_last)
    fulls = [
        pltpu.make_async_copy(NM.at[b], full_hbm.at[:, pl.ds(b * LANES, LANES)], full_sem.at[b]) for b in blocks
    ]
    for copy in fulls:
        copy.start()
    spread_sent(*spread0)
    for copy in mean_out + second_out:
        copy.wait_send()
    spread_sent(*spread_mean)
    spread_sent(*spread1)
    spread_sent(*spread_last)
    for copy in writes + fulls:
        copy.wait()
    inc_copy.wait()


def on_device(members, courant_x, courant_y, obs_cell, innovation, obs_weight, offsets, weights):
    n, rows, cols = members.shape
    groups = lax.axis_size(GROUP)
    n_grp = lax.axis_size("grp")
    assert cols == groups * LANES and rows % SUB == 0
    tall = rows + 2 * REACH
    deep = rows + 4 * SUB
    f32 = jnp.float32
    vmem = pltpu.VMEM
    dma = pltpu.SemaphoreType.DMA
    scratch = [
        vmem((n + 2, groups, deep, LANES), f32),
        vmem((5, groups, deep, LANES), f32),
        vmem((groups, deep, LANES), f32),
        vmem((groups, deep, LANES), f32),
        vmem((n + 2, groups, tall, LANES), f32),
        vmem((groups, tall, LANES), f32),
        vmem((groups, tall, LANES), f32),
        vmem((tall, LANES), f32),
        vmem((groups, tall, LANES), f32),
    ]
    scratch += [vmem((rows, LANES), f32)] * 4
    for _ in range(2):
        scratch += [vmem((groups, rows, LANES), f32), vmem((groups, SUB, LANES), f32), vmem((groups, SUB, LANES), f32)]
    scratch += [
        vmem((groups, tall, LANES), f32),
        vmem((len(SHIFTS), groups, tall + SUB, LANES), f32),
        vmem((len(SHIFTS), groups, tall, LANES), f32),
        vmem((groups, rows, LANES), f32),
        vmem((groups, rows, LANES), f32),
        vmem((rows, LANES), f32),
        vmem((groups, rows, LANES), f32),
        vmem((groups, rows, LANES), f32),
        vmem((rows, LANES), f32),
        vmem((groups, rows, LANES), f32),
        pltpu.SMEM((2, offsets.shape[0]), jnp.int32),
        pltpu.SMEM(weights.shape, f32),
        vmem(obs_cell.shape, jnp.int32),
        vmem(innovation.shape, f32),
        vmem(obs_weight.shape, f32),
        vmem((rows, LANES), f32),
        dma((6,)),
        vmem((n, groups, rows, LANES), f32),
        dma((groups,)),
        dma((3, groups)),
        dma((groups,)),
        dma((2, n + 2)),
        dma((2, n + 2)),
        dma((3, groups)),
        dma((3, groups)),
        dma((3, groups)),
        dma((3, groups)),
    ]
    scratch += [dma((1, groups))] * 10
    left = pl.BlockSpec(memory_space=pltpu.HBM)
    fields, block, full = pl.pallas_call(
        functools.partial(kernel, (n, rows, groups, n_grp)),
        out_shape=(
            jax.ShapeDtypeStruct(members.shape, f32),
            jax.ShapeDtypeStruct((rows, LANES), f32),
            jax.ShapeDtypeStruct((rows, cols), f32),
        ),
        in_specs=[left] * 8,
        out_specs=(left, left, left),
        scratch_shapes=scratch,
        compiler_params=pltpu.CompilerParams(collective_id=0, has_side_effects=True, vmem_limit_bytes=67043328),
        name="cycle",
    )(offsets.T, weights, members, courant_x, courant_y, obs_cell, innovation, obs_weight)
    return fields + full[None], block


def solution(mesh):
    placed = (
        P(GROUP, "tile", None),
        P("tile", None),
        P("tile", None),
        P("tile", GROUP, None),
        P("tile", GROUP, None),
        P("tile", GROUP, None),
        P(),
        P(),
    )
    return jax.shard_map(
        on_device,
        mesh=mesh,
        in_specs=placed,
        out_specs=(P(GROUP, "tile", None), P("tile", GROUP)),
        check_vma=False,
    )
```

```python
import functools
import math

import jax
import jax.numpy as jnp
from jax import lax
from jax.experimental import pallas as pl
from jax.experimental.pallas import tpu as pltpu
from jax.sharding import PartitionSpec as P

RADIUS = 2
FSTEPS = 3
STEP_SIZE = 0.25
GROUP = ("member", "grp")
MESH = pl.DeviceIdType.MESH
SUB = 8
LANES = 128
REACH = 2 * RADIUS
SHIFTS = tuple(range(-RADIUS, RADIUS + 1))


def remote(src, dst, send_sem, recv_sem, where):
    return pltpu.make_async_remote_copy(
        src_ref=src, dst_ref=dst, send_sem=send_sem, recv_sem=recv_sem, device_id=where, device_id_type=MESH
    )


def moved(blocks, c, lane):
    if c == 0:
        return blocks
    turned = [pltpu.roll(x, (-c) % LANES, 1) for x in blocks]
    nothing = jnp.zeros_like(blocks[0])
    out = []
    for b in range(len(blocks)):
        if c > 0:
            other = turned[b + 1] if b + 1 < len(blocks) else nothing
            out.append(jnp.where(lane >= LANES - c, other, turned[b]))
        else:
            other = turned[b - 1] if b > 0 else nothing
            out.append(jnp.where(lane < -c, other, turned[b]))
    return out


def kernel(
    shape,
    offs_hbm, wts_hbm, members, cx_hbm, cy_hbm, cell_hbm, innov_hbm, weight_hbm,
    out_hbm, inc_hbm, full_hbm,
    Q, C, T1, T2, D, OWN, MR, MB, MG, OBW, OBI, G0, G1,
    M0, U0, L0, M1, U1, L1, H, U, Z, ACC, XP, X0, R0, R1, NB, NM,
    offs, wts, cell_ref, innov_ref, weight_ref, inc_buf, small_sem,
    F, full_sem,
    in_sem, out_sem, hs, hr, s0, r0, s1, r1, sm1, rm1, sm2, rm2, sx0, rx0, sx1, rx1, sn, rn,
):
    n, rows, groups, n_grp = shape
    total = n * groups
    tiles = lax.axis_size("tile")
    tile = lax.axis_index("tile")
    me = lax.axis_index("member") * n_grp + lax.axis_index("grp")
    has_up = tile > 0
    has_down = tile < tiles - 1
    top = 2 * SUB
    tall = rows + 2 * REACH
    lane = lax.broadcasted_iota(jnp.int32, (SUB, LANES), 1)
    blocks = range(groups)

    def at(p, t=None):
        where = {"member": p // n_grp, "grp": lax.rem(p, n_grp)}
        if t is not None:
            where["tile"] = t
        return where

    def partner(d):
        return lax.rem(me + d, groups)

    def sender(d):
        return lax.rem(me + groups - d, groups)

    def loads():
        for b in blocks:
            cols = pl.ds(b * LANES, LANES)
            yield pltpu.make_async_copy(cx_hbm.at[:, cols], Q.at[n, b, pl.ds(top, rows)], in_sem.at[1, b])
            yield pltpu.make_async_copy(cy_hbm.at[:, cols], Q.at[n + 1, b, pl.ds(top, rows)], in_sem.at[2, b])
        for b in blocks:
            cols = pl.ds(b * LANES, LANES)
            yield pltpu.make_async_copy(members.at[:, :, cols], Q.at[pl.ds(0, n), b, pl.ds(top, rows)], in_sem.at[0, b])

    small = [
        pltpu.make_async_copy(a, b, small_sem.at[i])
        for i, (a, b) in enumerate(
            [(cell_hbm, cell_ref), (innov_hbm, innov_ref), (weight_hbm, weight_ref), (offs_hbm, offs), (wts_hbm, wts)]
        )
    ]
    for copy in small:
        copy.start()
    for copy in loads():
        copy.start()

    barrier = pltpu.get_barrier_semaphore()
    for d in range(1, groups):
        pl.semaphore_signal(barrier, inc=1, device_id=at(partner(d)), device_id_type=MESH)

    @pl.when(has_up)
    def _():
        for d in blocks:
            pl.semaphore_signal(barrier, inc=1, device_id=at(partner(d), tile - 1), device_id_type=MESH)

    @pl.when(has_down)
    def _():
        for d in blocks:
            pl.semaphore_signal(barrier, inc=1, device_id=at(partner(d), tile + 1), device_id_type=MESH)

    for copy in small:
        copy.wait()

    cell = cell_ref[0]
    w = weight_ref[0]
    wi = -w * innov_ref[0]
    count = cell.shape[1]
    row_of = cell // LANES
    col_of = cell % LANES
    pick_r = lax.broadcasted_iota(jnp.int32, (rows, count), 0) == row_of
    pick_c = (lax.broadcasted_iota(jnp.int32, (LANES, count), 0) == col_of).astype(jnp.float32)
    left = jnp.concatenate([jnp.where(pick_r, w, 0.0), jnp.where(pick_r, wi, 0.0)], axis=0)
    both = lax.dot_general(
        left, pick_c, (((1,), (1,)), ((), ())),
        precision=lax.Precision.HIGHEST, preferred_element_type=jnp.float32,
    )
    OBW[...] = both[:rows]
    OBI[...] = both[rows:]
    G0[...] = both[rows:]
    M0[me] = both[rows:]

    sides = jnp.where(has_up, 1, 0) + jnp.where(has_down, 1, 0)
    for m in range(3):
        @pl.when(sides == m)
        def _(m=m):
            pl.semaphore_wait(barrier, groups - 1 + m * groups)


    def up_copy(k):
        return remote(
            Q.at[k, :, pl.ds(top, SUB)], Q.at[k, :, pl.ds(top + rows, SUB)], hs.at[0, k], hr.at[0, k],
            {"tile": tile - 1},
        )

    def down_copy(k):
        return remote(
            Q.at[k, :, pl.ds(top + rows - SUB, SUB)], Q.at[k, :, pl.ds(top - SUB, SUB)], hs.at[1, k], hr.at[1, k],
            {"tile": tile + 1},
        )

    def halo_wait(k):
        @pl.when(has_down)
        def _():
            up_copy(k).wait_recv()

        @pl.when(has_up)
        def _():
            down_copy(k).wait_recv()

    blank = jnp.zeros((SUB, LANES), jnp.float32)

    @pl.when(jnp.logical_not(has_up))
    def _():
        for k in range(n + 2):
            for b in blocks:
                Q[k, b, pl.ds(top - SUB, SUB)] = blank
        for b in blocks:
            U0[b] = blank
            U1[b] = blank

    @pl.when(jnp.logical_not(has_down))
    def _():
        for k in range(n + 2):
            for b in blocks:
                Q[k, b, pl.ds(top + rows, SUB)] = blank
        for b in blocks:
            L0[b] = blank
            L1[b] = blank

    def spread_start(src, main, up, low, ssem, rsem, edges):
        for d in range(1, groups):
            remote(src, main.at[me], ssem.at[0, d], rsem.at[0, d], at(partner(d))).start()
        if edges:
            @pl.when(has_up)
            def _():
                for d in blocks:
                    remote(src.at[pl.ds(0, SUB)], low.at[me], ssem.at[1, d], rsem.at[1, d], at(partner(d), tile - 1)).start()

            @pl.when(has_down)
            def _():
                for d in blocks:
                    remote(src.at[pl.ds(rows - SUB, SUB)], up.at[me], ssem.at[2, d], rsem.at[2, d], at(partner(d), tile + 1)).start()

    def spread_recv(src, main, up, low, ssem, rsem, edges):
        for d in range(1, groups):
            remote(src, main.at[sender(d)], ssem.at[0, d], rsem.at[0, d], at(sender(d))).wait_recv()
        if edges:
            @pl.when(has_down)
            def _():
                for d in blocks:
                    remote(src.at[pl.ds(0, SUB)], low.at[sender(d)], ssem.at[1, d], rsem.at[1, d], at(sender(d))).wait_recv()

            @pl.when(has_up)
            def _():
                for d in blocks:
                    remote(src.at[pl.ds(0, SUB)], up.at[sender(d)], ssem.at[2, d], rsem.at[2, d], at(sender(d))).wait_recv()

    def spread_sent(src, main, up, low, ssem, rsem, edges):
        for d in range(1, groups):
            remote(src, main.at[me], ssem.at[0, d], rsem.at[0, d], at(partner(d))).wait_send()
        if edges:
            @pl.when(has_up)
            def _():
                for d in blocks:
                    remote(src.at[pl.ds(0, SUB)], low.at[me], ssem.at[1, d], rsem.at[1, d], at(partner(d), tile - 1)).wait_send()

            @pl.when(has_down)
            def _():
                for d in blocks:
                    remote(src.at[pl.ds(0, SUB)], up.at[me], ssem.at[2, d], rsem.at[2, d], at(partner(d), tile + 1)).wait_send()

    def deal(src, dst, ssem, rsem):
        return [
            remote(src.at[partner(d)], dst.at[me], ssem.at[0, d], rsem.at[0, d], at(partner(d)))
            for d in range(1, groups)
        ]

    def dealt_wait(src, dst, ssem, rsem):
        for d in range(1, groups):
            remote(src.at[0], dst.at[sender(d)], ssem.at[0, d], rsem.at[0, d], at(sender(d))).wait_recv()

    spread0 = (G0, M0, U0, L0, s0, r0, True)
    spread_start(*spread0)
    for copy in loads():
        copy.wait()

    order = [n, n + 1] + list(range(n))
    for k in order:
        @pl.when(has_up)
        def _(k=k):
            up_copy(k).start()

        @pl.when(has_down)
        def _(k=k):
            down_copy(k).start()


    halo_wait(n)
    halo_wait(n + 1)

    def coefficients(i, carry):
        r = pl.ds(pl.multiple_of(top - SUB + i * SUB, SUB), SUB)
        for b in blocks:
            cx = Q[n, b, r]
            cy = Q[n + 1, b, r]
            C[0, b, r] = 1.0 - jnp.abs(cx) - jnp.abs(cy)
            C[1, b, r] = jnp.maximum(cx, 0.0)
            C[2, b, r] = -jnp.minimum(cx, 0.0)
            C[3, b, r] = jnp.maximum(cy, 0.0)
            C[4, b, r] = -jnp.minimum(cy, 0.0)
        return carry

    lax.fori_loop(0, rows // SUB + 2, coefficients, 0)
    for i in range(tall // SUB):
        for b in blocks:
            OWN[b, pl.ds(i * SUB, SUB)] = blank

    entries = offs.shape[1]
    weights = [wts[s] for s in range(entries)]
    weight_sum = weights[0]
    for s in range(1, entries):
        weight_sum = weight_sum + weights[s]
    inverse = 1.0 / jnp.full((SUB, LANES), weight_sum, jnp.float32)
    scale = inverse * inverse * (-STEP_SIZE / (total - 1))
    first_row = tile * rows - RADIUS
    end_row = tiles * rows
    sub = lax.broadcasted_iota(jnp.int32, (SUB, LANES), 0)

    def assemble(main, up, low):
        for b in blocks:
            H[b, pl.ds(0, REACH)] = up[b, pl.ds(SUB - REACH, REACH)]
            H[b, pl.ds(REACH, rows)] = main[b]
            H[b, pl.ds(REACH + rows, REACH)] = low[b, pl.ds(0, REACH)]

    def clear():
        for i in range(rows // SUB):
            for b in blocks:
                ACC[b, pl.ds(i * SUB, SUB)] = blank

    def apply(k, carry):
        def lift(i, c1):
            r = pl.ds(pl.multiple_of(i * SUB, SUB), SUB)
            u = [D[k, b, r] * H[b, r] for b in blocks]
            for c in SHIFTS:
                v = moved(u, c, lane)
                for b in blocks:
                    U[c + RADIUS, b, r] = v[b]
            return c1

        lax.fori_loop(0, tall // SUB, lift, 0, unroll=True)

        def adjoint(i, c1):
            z = []
            place = first_row + i * SUB + sub
            keep = (place >= 0) & (place < end_row)
            for b in blocks:
                acc = None
                for s in range(entries):
                    part = weights[s] * U[RADIUS - offs[1, s], b, pl.ds(i * SUB + RADIUS - offs[0, s], SUB)]
                    acc = part if acc is None else acc + part
                z.append(jnp.where(keep, acc, 0.0))
            r = pl.ds(pl.multiple_of(i * SUB, SUB), SUB)
            for c in SHIFTS:
                v = moved(z, c, lane)
                for b in blocks:
                    Z[c + RADIUS, b, r] = v[b]
            return c1

        lax.fori_loop(0, tall // SUB, adjoint, 0, unroll=True)

        sign = jnp.where(k == n, -1.0, 1.0)

        def direct(i, c1):
            r = pl.ds(pl.multiple_of(i * SUB, SUB), SUB)
            for b in blocks:
                acc = None
                for s in range(entries):
                    part = weights[s] * Z[RADIUS + offs[1, s], b, pl.ds(i * SUB + RADIUS + offs[0, s], SUB)]
                    acc = part if acc is None else acc + part
                ACC[b, r] += (sign * D[k, b, pl.ds(i * SUB + REACH, SUB)]) * acc
            return c1

        lax.fori_loop(0, rows // SUB, direct, 0, unroll=True)
        return carry

    def publish(copies, dst):
        for i in range(rows // SUB):
            r = pl.ds(i * SUB, SUB)
            for b in blocks:
                XP[b, r] = ACC[b, r] * scale
        for copy in copies:
            copy.start()
        dst[me] = XP[me]

    def advect(get, first, i):
        base = first + i * SUB
        q = [get(b, base) for b in blocks]
        before = moved(q, -1, lane)
        after = moved(q, 1, lane)
        out = []
        for b in blocks:
            r = pl.ds(base, SUB)
            out.append(
                (C[0, b, r] * q[b] + C[1, b, r] * get(b, base - 1))
                + (C[2, b, r] * get(b, base + 1) + C[3, b, r] * before[b])
                + C[4, b, r] * after[b]
            )
        return out

    def forecast(k, carry):
        halo_wait(k)
        for i in range(rows // SUB + 2):
            new = advect(lambda b, r: Q[k, b, pl.ds(r, SUB)], top - SUB, i)
            for b in blocks:
                T1[b, pl.ds(top - SUB + i * SUB, SUB)] = new[b]
        for i in range(rows // SUB + 2):
            new = advect(lambda b, r: T1[b, pl.ds(r, SUB)], top - SUB, i)
            for b in blocks:
                T2[b, pl.ds(top - SUB + i * SUB, SUB)] = new[b]
        for i in range(tall // SUB):
            new = advect(lambda b, r: T2[b, pl.ds(r, SUB)], top - REACH, i)
            r = pl.ds(i * SUB, SUB)
            for b in blocks:
                D[k, b, r] = new[b]
        for b in blocks:
            F[k, b] = D[k, b, pl.ds(REACH, rows)]
        for i in range(tall // SUB):
            r = pl.ds(i * SUB, SUB)
            for b in blocks:
                gap = D[k, b, r] - D[0, b, r]
                D[k, b, r] = jnp.where(k > 0, gap, D[k, b, r])
                OWN[b, r] += gap * (1.0 / n)
        return carry

    lax.fori_loop(0, 2, forecast, 0)
    spread_recv(*spread0)
    assemble(M0, U0, L0)
    clear()
    steps = (n - 2) // 3

    def both_stages(j, carry):
        lax.fori_loop(3 * j + 2, 3 * j + 5, forecast, 0)
        return apply(j + 1, carry)

    lax.fori_loop(0, steps, both_stages, 0)
    lax.fori_loop(3 * steps + 2, n, forecast, 0)
    for i in range(tall // SUB):
        r = pl.ds(i * SUB, SUB)
        for b in blocks:
            gap = OWN[b, r]
            D[n, b, r] = gap * math.sqrt(n)
            OWN[b, r] = gap + D[0, b, r]
    writes = [
        pltpu.make_async_copy(F.at[:, b], out_hbm.at[:, :, pl.ds(b * LANES, LANES)], out_sem.at[b]) for b in blocks
    ]
    for copy in writes:
        copy.start()

    mean_out = deal(OWN, MR, sm1, rm1)
    for copy in mean_out:
        copy.start()
    MR[me] = OWN[me]

    for b in blocks:
        D[n + 1, b] = jnp.full((tall, LANES), math.sqrt((total - 1) / groups), jnp.float32)
    half = (steps + 1 + n + 2) // 2
    lax.fori_loop(steps + 1, half, apply, 0)
    dealt_wait(OWN, MR, sm1, rm1)
    mean = MR[0]
    for b in range(1, groups):
        mean = mean + MR[b]
    MB[...] = mean * (1.0 / groups)
    MG[me] = mean * (1.0 / groups)
    spread_mean = (MB, MG, None, None, sm2, rm2, False)
    spread_start(*spread_mean)
    lax.fori_loop(half, n + 2, apply, 0)
    spread_recv(*spread_mean)
    for b in blocks:
        D[n + 2, b] = (OWN[b] - MG[b]) * math.sqrt(n)
    lax.fori_loop(n + 2, n + 3, apply, 0)
    first_out = deal(XP, R0, sx0, rx0)
    publish(first_out, R0)
    dealt_wait(XP, R0, sx0, rx0)
    x0 = R0[0]
    for b in range(1, groups):
        x0 = x0 + R0[b]
    X0[...] = x0 * (1.0 - STEP_SIZE)
    g1 = OBW[...] * x0 + OBI[...]
    G1[...] = g1
    M1[me] = g1
    spread1 = (G1, M1, U1, L1, s1, r1, True)
    spread_start(*spread1)
    for copy in first_out:
        copy.wait_send()
    spread_recv(*spread1)
    assemble(M1, U1, L1)
    clear()
    lax.fori_loop(1, n + 3, apply, 0)
    second_out = deal(XP, R1, sx1, rx1)
    publish(second_out, R1)
    dealt_wait(XP, R1, sx1, rx1)
    block = X0[...]
    for b in blocks:
        block = block + R1[b]
    NB[...] = block
    NM[me] = block
    inc_buf[...] = block
    inc_copy = pltpu.make_async_copy(inc_buf, inc_hbm, small_sem.at[5])
    inc_copy.start()
    spread_last = (NB, NM, None, None, sn, rn, False)
    spread_start(*spread_last)

    for k in order:
        @pl.when(has_up)
        def _(k=k):
            up_copy(k).wait_send()

        @pl.when(has_down)
        def _(k=k):
            down_copy(k).wait_send()

    spread_recv(*spread_last)
    fulls = [
        pltpu.make_async_copy(NM.at[b], full_hbm.at[:, pl.ds(b * LANES, LANES)], full_sem.at[b]) for b in blocks
    ]
    for copy in fulls:
        copy.start()
    spread_sent(*spread0)
    for copy in mean_out + second_out:
        copy.wait_send()
    spread_sent(*spread_mean)
    spread_sent(*spread1)
    spread_sent(*spread_last)
    for copy in writes + fulls:
        copy.wait()
    inc_copy.wait()


def on_device(members, courant_x, courant_y, obs_cell, innovation, obs_weight, offsets, weights):
    n, rows, cols = members.shape
    groups = lax.axis_size(GROUP)
    n_grp = lax.axis_size("grp")
    assert cols == groups * LANES and rows % SUB == 0
    tall = rows + 2 * REACH
    deep = rows + 4 * SUB
    f32 = jnp.float32
    vmem = pltpu.VMEM
    dma = pltpu.SemaphoreType.DMA
    scratch = [
        vmem((n + 2, groups, deep, LANES), f32),
        vmem((5, groups, deep, LANES), f32),
        vmem((groups, deep, LANES), f32),
        vmem((groups, deep, LANES), f32),
        vmem((n + 3, groups, tall, LANES), f32),
        vmem((groups, tall, LANES), f32),
        vmem((groups, tall, LANES), f32),
        vmem((tall, LANES), f32),
        vmem((groups, tall, LANES), f32),
    ]
    scratch += [vmem((rows, LANES), f32)] * 4
    for _ in range(2):
        scratch += [vmem((groups, rows, LANES), f32), vmem((groups, SUB, LANES), f32), vmem((groups, SUB, LANES), f32)]
    scratch += [
        vmem((groups, tall, LANES), f32),
        vmem((len(SHIFTS), groups, tall + SUB, LANES), f32),
        vmem((len(SHIFTS), groups, tall, LANES), f32),
        vmem((groups, rows, LANES), f32),
        vmem((groups, rows, LANES), f32),
        vmem((rows, LANES), f32),
        vmem((groups, rows, LANES), f32),
        vmem((groups, rows, LANES), f32),
        vmem((rows, LANES), f32),
        vmem((groups, rows, LANES), f32),
        pltpu.SMEM((2, offsets.shape[0]), jnp.int32),
        pltpu.SMEM(weights.shape, f32),
        vmem(obs_cell.shape, jnp.int32),
        vmem(innovation.shape, f32),
        vmem(obs_weight.shape, f32),
        vmem((rows, LANES), f32),
        dma((6,)),
        vmem((n, groups, rows, LANES), f32),
        dma((groups,)),
        dma((3, groups)),
        dma((groups,)),
        dma((2, n + 2)),
        dma((2, n + 2)),
        dma((3, groups)),
        dma((3, groups)),
        dma((3, groups)),
        dma((3, groups)),
    ]
    scratch += [dma((1, groups))] * 10
    left = pl.BlockSpec(memory_space=pltpu.HBM)
    fields, block, full = pl.pallas_call(
        functools.partial(kernel, (n, rows, groups, n_grp)),
        out_shape=(
            jax.ShapeDtypeStruct(members.shape, f32),
            jax.ShapeDtypeStruct((rows, LANES), f32),
            jax.ShapeDtypeStruct((rows, cols), f32),
        ),
        in_specs=[left] * 8,
        out_specs=(left, left, left),
        scratch_shapes=scratch,
        compiler_params=pltpu.CompilerParams(collective_id=0, has_side_effects=True, vmem_limit_bytes=67043328),
        name="cycle",
    )(offsets.T, weights, members, courant_x, courant_y, obs_cell, innovation, obs_weight)
    return fields + full[None], block


def solution(mesh):
    placed = (
        P(GROUP, "tile", None),
        P("tile", None),
        P("tile", None),
        P("tile", GROUP, None),
        P("tile", GROUP, None),
        P("tile", GROUP, None),
        P(),
        P(),
    )
    return jax.shard_map(
        on_device,
        mesh=mesh,
        in_specs=placed,
        out_specs=(P(GROUP, "tile", None), P("tile", GROUP)),
        check_vma=False,
    )
```
